32 devices in a mesh: row: 8 (over y, x, core), col: 4 (over z).
Axes of the slice: x: 2, y: 2, z: 4, core: 2. Of those that a mesh axis runs over, the one named last changes fastest.
Arguments:
- vector: float32 [4096, 4096], P('row', 'col'), may hold values from -6 to 6
- one_electron: float32 [16, 16], replicated, may hold values from -0.18 to 0.18
- links: int32 [32, 8], replicated, may hold values from 0 to 31, as said below
- counts: int32 [32], replicated, may hold values from 4 to 8, as said below
- pairs: int32 [32, 8], P('row'), may hold values from 0 to 255
- signs: int32 [32, 8, 128, 128], P('row'), may hold values from -1 to 1
Outputs:
- sigma_vector: float32 [4096, 4096], P('row', 'col')
The draws below stay inside these ranges and needn't reach their ends.
Inputs may be any that keep to these rules, and one draw needn't show every extreme that they name: `links`: entries name string blocks; only the first counts[I] entries of block I are used. Counting used entries only, the blocks I with I // 4 = d name blocks K with K // 4 = s at most 4 times for any d and s, and some pair d, s reaches 4. Block I has counts[I] used links; every block I with I % 4 = 0 has 8.
All inputs are finite; a program needn't handle non-finite values.
Results may differ from the reference program's by a relative error of at most 0.000051.
Values sent between devices are 32-bit elements; how exact they have to be, the bound alone decides.
A program may use at most 128 MiB of HBM per device.

```python
import jax
import jax.numpy as jnp
from jax import lax

BLK = 128
NORB = 16
LMAX = 8
A_DEV = 4
NPAIR = 256
NBLK_A = 32
NA = 4096


def link_tables(key, salt, blocks_all, blocks_dev, link_max):
    key = jax.random.fold_in(key, salt)
    count_key, order_key, local_key = jax.random.split(key, 3)
    devices = blocks_all // blocks_dev
    slot_width = blocks_dev * link_max
    capacity = (slot_width + devices - 1) // devices
    used = jax.random.randint(count_key, (blocks_all,), link_max // 2, link_max + 1)
    first_block = jnp.arange(blocks_all, dtype=jnp.int32) % blocks_dev == 0
    used = jnp.where(first_block, link_max, used).astype(jnp.int32)
    in_use = (jnp.arange(link_max, dtype=jnp.int32)[None, :] < used[:, None]).reshape(devices, slot_width)
    position = jnp.cumsum(in_use.astype(jnp.int32), axis=1) - 1
    position = jnp.clip(position, 0, slot_width - 1)

    def one_order(order_seed):
        return jax.random.permutation(order_seed, devices)
    orders = jax.vmap(one_order)(jax.random.split(order_key, devices)).astype(jnp.int32)
    sources = jnp.take_along_axis(orders, position // capacity, axis=1)
    local_block = jax.random.randint(local_key, (devices, slot_width), 0, blocks_dev)
    link_table = (sources * blocks_dev + local_block).reshape(blocks_all, link_max)
    return (link_table.astype(jnp.int32), used)


def draw_links(key, part):
    return link_tables(key, 11, NBLK_A, A_DEV, LMAX)[0]


def draw_counts(key, part):
    return link_tables(key, 11, NBLK_A, A_DEV, LMAX)[1]


def with_ends(result, key, low, largest):
    longest = result.shape.index(max(result.shape))
    spots = []
    for shift in (0, 1):
        where = [jax.random.randint(jax.random.fold_in(key, axis), (), 0, length) for axis, length in enumerate(result.shape)]
        where[longest] = (where[longest] + shift) % result.shape[longest]
        spots.append(tuple(where))
    return result.at[spots[0]].set(low).at[spots[1]].set(largest)


def steps_of(stream_key, dims, shards, least, largest):
    level, own = 1.0, jax.random.fold_in(stream_key, 6)
    for dim, blocks in shards:
        steps = jnp.exp(jax.random.uniform(jax.random.fold_in(own, dim), (blocks,), jnp.float32, least / len(shards), largest / len(shards)))
        level = level * jnp.repeat(steps, dims[dim] // blocks).reshape([-1 if axis == dim else 1 for axis in range(len(dims))])
    return level


def noise(stream_key, shape, scale, reach, shards=(), held_as=jnp.bfloat16):
    result = scale * jax.random.normal(stream_key, shape, jnp.float32)
    if shards:
        result = result * steps_of(stream_key, shape, shards, -0.22, 0.18)
    return jnp.clip(result, -reach, reach).astype(held_as)


def setup_inputs(seed: int = 0) -> dict:
    seeds = jax.random.split(jax.random.key(seed), 7)
    return {
        "vector": noise(seeds[0], (NA, NA), 1.0, 6.0, ((0, 8), (1, 4)), jnp.float32),
        "one_electron": noise(seeds[1], (NORB, NORB), 0.03, 0.18, (), jnp.float32),
        "links": draw_links(jax.random.fold_in(seeds[6], 71), 0),
        "counts": draw_counts(jax.random.fold_in(seeds[6], 71), 0),
        "pairs": with_ends(jax.random.randint(seeds[4], (NBLK_A, LMAX), 0, NPAIR), jax.random.fold_in(seeds[4], 1), 0, NPAIR - 1).astype(jnp.int32),
        "signs": with_ends(jax.random.randint(seeds[5], (NBLK_A, LMAX, BLK, BLK), -1, 2), jax.random.fold_in(seeds[5], 1), -1, 1).astype(jnp.int32),
    }


def pair_values(pair_ids, used, integrals):
    flat_table = integrals.reshape(-1)
    values = flat_table[pair_ids]
    in_use = jnp.arange(pair_ids.shape[1], dtype=jnp.int32)[None, :] < used[:, None]
    return jnp.where(in_use, values, jnp.zeros_like(values))


def reference(vector, one_electron, links, counts, pairs, signs):
    replace = pair_values(pairs, counts, one_electron)[:, :, None, None] * signs.astype(jnp.float32)
    row_tiles = vector.reshape(NBLK_A, BLK, NA)
    column_blocks = vector.reshape(NA, NBLK_A, BLK)

    def alpha_block(inputs):
        link_row, replace_row = inputs
        fetched = row_tiles[link_row]
        return jnp.einsum("lmk,lkb->mb", replace_row, fetched, precision=lax.Precision.HIGHEST)

    def beta_block(inputs):
        link_row, replace_row = inputs
        fetched = column_blocks[:, link_row, :]
        return jnp.einsum("alk,lmk->am", fetched, replace_row, precision=lax.Precision.HIGHEST)

    sigma_alpha = lax.map(alpha_block, (links, replace)).reshape(NA, NA)
    sigma_beta = lax.map(beta_block, (links, replace))
    sigma_beta = jnp.transpose(sigma_beta, (1, 0, 2)).reshape(NA, NA)
    return sigma_alpha + sigma_beta
```

```python
import functools

import jax
import jax.numpy as jnp
from jax import lax
from jax.experimental import pallas as pl
from jax.experimental.pallas import tpu as pltpu
from jax.sharding import PartitionSpec as P

MESH = pl.DeviceIdType.MESH
PARTS_A = 4
PARTS_B = 4
PAD = 8


def pair_values(pair_ids, used, integrals):
    flat_table = integrals.reshape(-1)
    onehot = pair_ids[:, :, None] == jnp.arange(flat_table.shape[0], dtype=jnp.int32)[None, None, :]
    values = jnp.sum(jnp.where(onehot, flat_table[None, None, :], 0.0), axis=2)
    in_use = jnp.arange(pair_ids.shape[1], dtype=jnp.int32)[None, :] < used[:, None]
    return jnp.where(in_use, values, 0.0)


def split(value):
    high = value.astype(jnp.bfloat16)
    low = (value - high.astype(jnp.float32)).astype(jnp.bfloat16)
    return high, low


def kernel(rows, cols, blocks, link_max, links, v, tab, out, *scratch):
    scratch = list(scratch)
    colbuf = [scratch.pop(0) for _ in range(PARTS_A)]
    rowbuf = [scratch.pop(0) for _ in range(PARTS_B)]
    own_tab, beta_tab, alpha_signs, beta_signs = scratch[:4]
    asend, arecv, bsend, brecv, tsend, trecv, lsem = scratch[4:]

    size = own_tab.shape[2]
    width = out.shape[1]
    wide = width // PARTS_A
    tall = out.shape[0] // PARTS_B
    spread = rows // cols
    blocks_b = blocks * spread
    tables = blocks * link_max
    chips = rows // 2
    reach = chips // 2
    across = chips // 2

    r = lax.axis_index("row")
    c = lax.axis_index("col")
    core = lax.rem(r, 2)
    chip = r // 2
    other = r + 1 - 2 * core
    place = jnp.where(chip < across, chip, chips - 1 - (chip - across))

    def chip_at(position):
        position = lax.rem(position + 2 * chips, chips)
        return jnp.where(position < across, position, across + (chips - 1 - position))

    def row_at(position, k):
        return 2 * chip_at(position) + k

    right = (row_at(place + 1, core), c)
    left = (row_at(place - 1, core), c)
    partner = (other, c)
    up = (r, jnp.minimum(c + 1, cols - 1))
    down = (r, jnp.maximum(c - 1, 0))
    has_up = c < cols - 1
    has_down = c > 0

    barrier = pltpu.get_barrier_semaphore()
    for device in (right, left, partner):
        pl.semaphore_signal(barrier, inc=1, device_id=device, device_id_type=MESH)

    @pl.when(has_up)
    def _():
        pl.semaphore_signal(barrier, inc=1, device_id=up, device_id_type=MESH)

    @pl.when(has_down)
    def _():
        pl.semaphore_signal(barrier, inc=1, device_id=down, device_id_type=MESH)

    loads = []
    for j in range(PARTS_A):
        for i in range(blocks):
            loads.append(pltpu.make_async_copy(
                v.at[pl.ds(i * size, size), pl.ds(j * wide, wide)],
                colbuf[j].at[r * blocks + i], lsem.at[len(loads)]))
    for i in range(PARTS_B):
        for k in range(blocks_b):
            loads.append(pltpu.make_async_copy(
                v.at[pl.ds(i * tall, tall), pl.ds(k * size, size)],
                rowbuf[i].at[c * blocks_b + k], lsem.at[len(loads)]))
    loads.append(pltpu.make_async_copy(tab, own_tab, lsem.at[len(loads)]))
    for load in loads:
        load.start()
    for load in loads:
        load.wait()

    pl.semaphore_wait(barrier, 3 + has_up.astype(jnp.int32) + has_down.astype(jnp.int32))

    pending = []

    def send(src, dst, ssem, rsem, device, cond=None):
        copy = pltpu.make_async_remote_copy(
            src_ref=src, dst_ref=dst, send_sem=ssem, recv_sem=rsem,
            device_id=device, device_id_type=MESH)
        pending.append((cond, copy))
        if cond is None:
            copy.start()
        else:
            pl.when(cond)(copy.start)

    def arrive(ref, ssem, rsem, cond=None):
        copy = pltpu.make_async_remote_copy(
            src_ref=ref, dst_ref=ref, send_sem=ssem, recv_sem=rsem,
            device_id=partner, device_id_type=MESH)
        if cond is None:
            copy.wait_recv()
        else:
            pl.when(cond)(copy.wait_recv)

    def alpha_part(j, position, k, t, leftward):
        start = row_at(position, k) * blocks
        count = blocks
        if t == reach - 1:
            count = blocks // 2
            if leftward:
                start = start + count
        return colbuf[j].at[pl.ds(start, count)]

    def alpha_send(j, t):
        ref = alpha_part(j, place - t, core, t, False)
        send(ref, ref, asend.at[j, t], arecv.at[j, t], right)
        ref = alpha_part(j, place + t, core, t, True)
        send(ref, ref, asend.at[j, reach + t], arecv.at[j, reach + t], left)

    def alpha_arrive(j, t):
        m = chips + 1 + t
        ref = alpha_part(j, place - 1 - t, core, t, False)
        arrive(ref, asend.at[j, t], arecv.at[j, t])
        send(ref, ref, asend.at[j, m], arecv.at[j, m], partner)
        m = m + reach
        ref = alpha_part(j, place + 1 + t, core, t, True)
        arrive(ref, asend.at[j, reach + t], arecv.at[j, reach + t])
        send(ref, ref, asend.at[j, m], arecv.at[j, m], partner)

    def alpha_partner(j):
        m = chips
        ref = colbuf[j].at[pl.ds(other * blocks, blocks)]
        arrive(ref, asend.at[j, m], arecv.at[j, m])
        for t in range(reach):
            m = chips + 1 + t
            arrive(alpha_part(j, place - 1 - t, 1 - core, t, False), asend.at[j, m], arecv.at[j, m])
            m = m + reach
            arrive(alpha_part(j, place + 1 + t, 1 - core, t, True), asend.at[j, m], arecv.at[j, m])

    def beta_part(i, tile):
        return rowbuf[i].at[pl.ds(jnp.clip(tile, 0, cols - 1) * blocks_b, blocks_b)]

    def beta_send(i, t):
        ref = beta_part(i, c - t)
        send(ref, ref, bsend.at[i, t], brecv.at[i, t], up, has_up & (c - t >= 0))
        ref = beta_part(i, c + t)
        m = cols - 1 + t
        send(ref, ref, bsend.at[i, m], brecv.at[i, m], down, has_down & (c + t < cols))

    def beta_arrive(i, t):
        arrive(beta_part(i, c - 1 - t), bsend.at[i, t], brecv.at[i, t], c - 1 - t >= 0)
        m = cols - 1 + t
        arrive(beta_part(i, c + 1 + t), bsend.at[i, m], brecv.at[i, m], c + 1 + t < cols)

    half = tables // 2

    def table_places(s):
        source = c * spread + s
        source_chip = source // 2
        source_place = jnp.where(
            source_chip < across, source_chip, chips - 1 - (source_chip - across))
        distance = lax.rem(place - source_place + chips, chips)
        return lax.rem(source, 2), distance

    def table_stage(s, first):
        source_core, distance = table_places(s)
        mine = core == source_core
        back = lax.rem(chips - distance, chips)
        at_source = mine & (distance == 0)
        for h in range(2):
            ref = beta_tab.at[s, pl.ds(h * half, half)]
            if first:
                here = at_source
                src = own_tab.at[pl.ds(h * half, half)]
            else:
                here = mine & (distance != 0)
                src = ref
                arrive(ref, tsend.at[s, h, 0], trecv.at[s, h], here)
            limit = reach if h == 0 else reach - 1
            other_limit = reach - 1 if h == 0 else reach
            go_right = here & (distance + 1 <= limit)
            go_left = here & (back + 1 <= other_limit)
            base = 0 if first else 3
            send(src, ref, tsend.at[s, h, base], trecv.at[s, h], right, go_right)
            send(src, ref, tsend.at[s, h, base + 1], trecv.at[s, h], left, go_left)
            send(src, ref, tsend.at[s, h, base + 2], trecv.at[s, h], partner, here)

    def table_finish(s):
        source_core, distance = table_places(s)
        mine = core == source_core
        for h in range(2):
            ref = beta_tab.at[s, pl.ds(h * half, half)]
            arrive(ref, tsend.at[s, h, 0], trecv.at[s, h], jnp.logical_not(mine))

    for j in range(PARTS_A):
        alpha_send(j, 0)
        ref = colbuf[j].at[pl.ds(r * blocks, blocks)]
        send(ref, ref, asend.at[j, chips], arecv.at[j, chips], partner)
        if j < PARTS_B:
            beta_send(j, 0)
    for i in range(PARTS_A, PARTS_B):
        beta_send(i, 0)
    for s in range(spread):
        table_stage(s, True)

    @pl.loop(0, tables)
    def _(index):
        signs = own_tab[index, :size, :].astype(jnp.bfloat16)
        alpha_signs[index] = jnp.concatenate([signs, signs], axis=1)

    def alpha_compute(j):
        @pl.loop(0, blocks)
        def _(block):
            total = jnp.zeros((size, wide), jnp.float32)
            for l in range(link_max):
                source = links[r * blocks + block, l]
                high, low = split(colbuf[j][source])
                index = block * link_max + l
                term = jnp.dot(alpha_signs[index], jnp.concatenate([high, low], axis=0),
                               preferred_element_type=jnp.float32)
                scale = own_tab[index, pl.ds(size, 1), :]
                scale = jnp.concatenate([scale] * (wide // size), axis=1)
                total = total + term * scale
            out[pl.ds(pl.multiple_of(block * size, size), size), pl.ds(j * wide, wide)] = total

    def beta_compute(i):
        @pl.loop(0, blocks_b)
        def _(block):
            total = jnp.zeros((tall, size), jnp.float32)
            for l in range(link_max):
                source = links[c * blocks_b + block, l]
                high, low = split(rowbuf[i][source])
                index = block * link_max + l
                term = lax.dot_general(
                    jnp.concatenate([high, low], axis=1), beta_signs[index],
                    (((1,), (1,)), ((), ())), preferred_element_type=jnp.float32)
                scale = beta_tab[block // blocks, lax.rem(index, tables), pl.ds(size, 1), :]
                total = total + term * scale
            where = (pl.ds(i * tall, tall), pl.ds(pl.multiple_of(block * size, size), size))
            out[where] = out[where] + total

    for t in range(1, max(reach, cols - 1) + 1):
        for j in range(max(PARTS_A, PARTS_B)):
            if j < PARTS_A and t <= reach:
                alpha_arrive(j, t - 1)
                if t < reach:
                    alpha_send(j, t)
            if j < PARTS_B and t < cols - 1:
                beta_arrive(j, t - 1)
                beta_send(j, t)
            if t == 1 and j == PARTS_A - 1:
                for s in range(spread):
                    table_stage(s, False)
            if t == reach and j < PARTS_A:
                if j > 0:
                    alpha_partner(j - 1)
                    alpha_compute(j - 1)
        if t == reach:
            alpha_partner(PARTS_A - 1)
            alpha_compute(PARTS_A - 1)
            for s in range(spread):
                source_core, distance = table_places(s)

                @pl.when((core == source_core) & (distance == 0))
                def _():
                    copy = pltpu.make_async_copy(own_tab, beta_tab.at[s], lsem.at[0])
                    copy.start()
                    copy.wait()

                table_finish(s)

                @pl.loop(0, tables)
                def _(index):
                    signs = beta_tab[s, index, :size, :].astype(jnp.bfloat16)
                    beta_signs[s * tables + index] = jnp.concatenate([signs, signs], axis=1)

    for i in range(PARTS_B):
        beta_arrive(i, cols - 2)
        beta_compute(i)

    for cond, copy in pending:
        if cond is None:
            copy.wait_send()
        else:
            pl.when(cond)(copy.wait_send)


def local(vector, one_electron, links, counts, pairs, signs, rows, cols):
    blocks, link_max = pairs.shape
    size = signs.shape[2]
    high, width = vector.shape
    spread = rows // cols
    tables = blocks * link_max
    used = lax.dynamic_slice_in_dim(counts, lax.axis_index("row") * blocks, blocks)
    coef = pair_values(pairs, used, one_electron).reshape(tables, 1, 1)
    tab = jnp.concatenate(
        [signs.reshape(tables, size, size).astype(jnp.float32),
         jnp.broadcast_to(coef, (tables, PAD, size))], axis=1)
    chips = rows // 2
    scratch = [pltpu.VMEM((rows * blocks, size, width // PARTS_A), jnp.float32)] * PARTS_A
    scratch += [pltpu.VMEM((cols * blocks * spread, high // PARTS_B, size), jnp.float32)] * PARTS_B
    scratch += [
        pltpu.VMEM((tables, size + PAD, size), jnp.float32),
        pltpu.VMEM((spread, tables, size + PAD, size), jnp.float32),
        pltpu.VMEM((tables, size, 2 * size), jnp.bfloat16),
        pltpu.VMEM((spread * tables, size, 2 * size), jnp.bfloat16),
        pltpu.SemaphoreType.DMA((PARTS_A, 2 * chips + 1)),
        pltpu.SemaphoreType.DMA((PARTS_A, 2 * chips + 1)),
        pltpu.SemaphoreType.DMA((PARTS_B, 2 * cols - 2)),
        pltpu.SemaphoreType.DMA((PARTS_B, 2 * cols - 2)),
        pltpu.SemaphoreType.DMA((spread, 2, 6)),
        pltpu.SemaphoreType.DMA((spread, 2)),
        pltpu.SemaphoreType.DMA((PARTS_A * blocks + PARTS_B * blocks * spread + 1,)),
    ]
    return pl.pallas_call(
        functools.partial(kernel, rows, cols, blocks, link_max),
        out_shape=jax.ShapeDtypeStruct(vector.shape, jnp.float32),
        in_specs=[
            pl.BlockSpec(memory_space=pltpu.SMEM),
            pl.BlockSpec(memory_space=pl.ANY),
            pl.BlockSpec(memory_space=pl.ANY),
        ],
        out_specs=pl.BlockSpec(memory_space=pltpu.VMEM),
        scratch_shapes=scratch,
        compiler_params=pltpu.CompilerParams(
            collective_id=0, has_side_effects=True, vmem_limit_bytes=60 << 20),
    )(links, vector, tab)


def solution(mesh):
    in_specs = (P("row", "col"), P(), P(), P(), P("row", None), P("row", None, None, None))
    out_specs = P("row", "col")
    body = functools.partial(local, rows=mesh.shape["row"], cols=mesh.shape["col"])
    return jax.shard_map(body, mesh=mesh, in_specs=in_specs, out_specs=out_specs, check_vma=False)
```

```python
import functools

import jax
import jax.numpy as jnp
from jax import lax
from jax.experimental import pallas as pl
from jax.experimental.pallas import tpu as pltpu
from jax.sharding import PartitionSpec as P

MESH = pl.DeviceIdType.MESH
PARTS_A = 4
PARTS_B = 4
PAD = 8
PIECES = 4


def pair_values(pair_ids, used, integrals):
    flat_table = integrals.reshape(-1)
    onehot = pair_ids[:, :, None] == jnp.arange(flat_table.shape[0], dtype=jnp.int32)[None, None, :]
    values = jnp.sum(jnp.where(onehot, flat_table[None, None, :], 0.0), axis=2)
    in_use = jnp.arange(pair_ids.shape[1], dtype=jnp.int32)[None, :] < used[:, None]
    return jnp.where(in_use, values, 0.0)


def split(value):
    high = value.astype(jnp.bfloat16)
    low = (value - high.astype(jnp.float32)).astype(jnp.bfloat16)
    return high, low


def kernel(rows, cols, blocks, link_max, links, v, tab, out, *scratch):
    scratch = list(scratch)
    colbuf = [scratch.pop(0) for _ in range(PARTS_A)]
    rowbuf = [scratch.pop(0) for _ in range(PARTS_B)]
    own_tab, beta_tab, help_tab, alpha_signs, beta_signs, help_signs, shared = scratch[:7]
    asend, arecv, bsend, brecv, tsend, trecv, hsend, hrecv, rsend, rrecv, lsem = scratch[7:]

    size = own_tab.shape[2]
    width = out.shape[1]
    wide = width // PARTS_A
    tall = out.shape[0] // PARTS_B
    spread = rows // cols
    blocks_b = blocks * spread
    tables = blocks * link_max
    chips = rows // 2
    reach = chips // 2
    across = chips // 2
    helped = PARTS_B // 2 if cols >= 4 else 0

    r = lax.axis_index("row")
    c = lax.axis_index("col")
    core = lax.rem(r, 2)
    chip = r // 2
    other = r + 1 - 2 * core
    place = jnp.where(chip < across, chip, chips - 1 - (chip - across))

    def chip_at(position):
        position = lax.rem(position + 2 * chips, chips)
        return jnp.where(position < across, position, across + (chips - 1 - position))

    def row_at(position, k):
        return 2 * chip_at(position) + k

    right = (row_at(place + 1, core), c)
    left = (row_at(place - 1, core), c)
    partner = (other, c)
    up = (r, jnp.minimum(c + 1, cols - 1))
    down = (r, jnp.maximum(c - 1, 0))
    has_up = c < cols - 1
    has_down = c > 0
    at_end = (c == 0) | (c == cols - 1)
    inner = jnp.logical_not(at_end)
    helper = (c == 1) | (c == cols - 2)
    aided = jnp.where(c == 1, 0, cols - 1)
    inward = jnp.where(c == 0, 1, cols - 2)

    barrier = pltpu.get_barrier_semaphore()
    for device in (right, left, partner):
        pl.semaphore_signal(barrier, inc=1, device_id=device, device_id_type=MESH)

    @pl.when(has_up)
    def _():
        pl.semaphore_signal(barrier, inc=1, device_id=up, device_id_type=MESH)

    @pl.when(has_down)
    def _():
        pl.semaphore_signal(barrier, inc=1, device_id=down, device_id_type=MESH)

    loads = []
    for j in range(PARTS_A):
        for i in range(blocks):
            loads.append(pltpu.make_async_copy(
                v.at[pl.ds(i * size, size), pl.ds(j * wide, wide)],
                colbuf[j].at[r * blocks + i], lsem.at[len(loads)]))
    for i in range(PARTS_B):
        for k in range(blocks_b):
            loads.append(pltpu.make_async_copy(
                v.at[pl.ds(i * tall, tall), pl.ds(k * size, size)],
                rowbuf[i].at[c * blocks_b + k], lsem.at[len(loads)]))
    loads.append(pltpu.make_async_copy(tab, own_tab, lsem.at[len(loads)]))
    for load in loads:
        load.start()
    for load in loads:
        load.wait()

    pl.semaphore_wait(barrier, 3 + has_up.astype(jnp.int32) + has_down.astype(jnp.int32))

    pending = []

    def send(src, dst, ssem, rsem, device, cond=None):
        copy = pltpu.make_async_remote_copy(
            src_ref=src, dst_ref=dst, send_sem=ssem, recv_sem=rsem,
            device_id=device, device_id_type=MESH)
        pending.append((cond, copy))
        if cond is None:
            copy.start()
        else:
            pl.when(cond)(copy.start)

    def arrive(ref, ssem, rsem, cond=None):
        copy = pltpu.make_async_remote_copy(
            src_ref=ref, dst_ref=ref, send_sem=ssem, recv_sem=rsem,
            device_id=partner, device_id_type=MESH)
        if cond is None:
            copy.wait_recv()
        else:
            pl.when(cond)(copy.wait_recv)

    def alpha_part(j, position, k, t, leftward):
        start = row_at(position, k) * blocks
        count = blocks
        if t == reach - 1:
            count = blocks // 2
            if leftward:
                start = start + count
        return colbuf[j].at[pl.ds(start, count)]

    def alpha_send(j, t):
        ref = alpha_part(j, place - t, core, t, False)
        send(ref, ref, asend.at[j, t], arecv.at[j, t], right)
        ref = alpha_part(j, place + t, core, t, True)
        send(ref, ref, asend.at[j, reach + t], arecv.at[j, reach + t], left)

    def alpha_arrive(j, t):
        m = chips + 1 + t
        ref = alpha_part(j, place - 1 - t, core, t, False)
        arrive(ref, asend.at[j, t], arecv.at[j, t])
        send(ref, ref, asend.at[j, m], arecv.at[j, m], partner)
        m = m + reach
        ref = alpha_part(j, place + 1 + t, core, t, True)
        arrive(ref, asend.at[j, reach + t], arecv.at[j, reach + t])
        send(ref, ref, asend.at[j, m], arecv.at[j, m], partner)

    def alpha_partner(j):
        m = chips
        ref = colbuf[j].at[pl.ds(other * blocks, blocks)]
        arrive(ref, asend.at[j, m], arecv.at[j, m])
        for t in range(reach):
            m = chips + 1 + t
            arrive(alpha_part(j, place - 1 - t, 1 - core, t, False), asend.at[j, m], arecv.at[j, m])
            m = m + reach
            arrive(alpha_part(j, place + 1 + t, 1 - core, t, True), asend.at[j, m], arecv.at[j, m])

    def beta_part(i, tile):
        return rowbuf[i].at[pl.ds(jnp.clip(tile, 0, cols - 1) * blocks_b, blocks_b)]

    def in_turn(i, tile, late):
        if i < helped or helped == 0:
            return jnp.bool_(not late) & (tile >= 0) & (tile < cols)
        from_end = (tile == 0) | (tile == cols - 1)
        return from_end if late else (tile > 0) & (tile < cols - 1)

    def beta_send(i, t, late):
        if late and (i < helped or helped == 0):
            return
        above = has_up & in_turn(i, c - t, late)
        below = has_down & in_turn(i, c + t, late)
        if i < helped:
            above = above & (c + 1 < cols - 1)
            below = below & (c - 1 > 0)
        ref = beta_part(i, c - t)
        m = 2 * late * (cols - 1) + t
        send(ref, ref, bsend.at[i, m], brecv.at[i, m], up, above)
        ref = beta_part(i, c + t)
        m = m + cols - 1
        send(ref, ref, bsend.at[i, m], brecv.at[i, m], down, below)

    def beta_arrive(i, t, late):
        if late and (i < helped or helped == 0):
            return
        above = in_turn(i, c - 1 - t, late)
        below = in_turn(i, c + 1 + t, late)
        if i < helped:
            above = above & inner
            below = below & inner
        m = 2 * late * (cols - 1) + t
        arrive(beta_part(i, c - 1 - t), bsend.at[i, m], brecv.at[i, m], above)
        m = m + cols - 1
        arrive(beta_part(i, c + 1 + t), bsend.at[i, m], brecv.at[i, m], below)

    def table_places(s):
        source = c * spread + s
        source_chip = source // 2
        source_place = jnp.where(
            source_chip < across, source_chip, chips - 1 - (source_chip - across))
        distance = lax.rem(place - source_place + chips, chips)
        return lax.rem(source, 2), distance

    piece = tables // (2 * PIECES)

    def table_stage(s, q, first):
        source_core, distance = table_places(s)
        mine = core == source_core
        at_source = mine & (distance == 0)
        for h in range(2):
            ref = beta_tab.at[s, pl.ds((h * PIECES + q) * piece, piece)]
            if first:
                here = at_source
                src = own_tab.at[pl.ds((h * PIECES + q) * piece, piece)]
            else:
                here = mine & (distance != 0)
                src = ref
                arrive(ref, tsend.at[s, h, q, 0], trecv.at[s, h, q], here)
            hops = distance if h == 0 else lax.rem(chips - distance, chips)
            onward = here & (hops + 1 < chips)
            base = 0 if first else 2
            device = right if h == 0 else left
            send(src, ref, tsend.at[s, h, q, base], trecv.at[s, h, q], device, onward)
            send(src, ref, tsend.at[s, h, q, base + 1], trecv.at[s, h, q], partner, here)

    def table_finish(s):
        source_core, distance = table_places(s)
        mine = core == source_core
        for q in range(PIECES):
            for h in range(2):
                ref = beta_tab.at[s, pl.ds((h * PIECES + q) * piece, piece)]
                arrive(ref, tsend.at[s, h, q, 0], trecv.at[s, h, q], jnp.logical_not(mine))

        @pl.when(mine & (distance == 0))
        def _():
            copy = pltpu.make_async_copy(own_tab, beta_tab.at[s], lsem.at[0])
            copy.start()
            copy.wait()

    half = tables // 2

    def help_send(s):
        for h in range(2):
            ref = pl.ds(h * half, half)
            send(beta_tab.at[s, ref], help_tab.at[s, ref], hsend.at[s, h, 0], hrecv.at[s, h],
                 (r, inward), at_end & (core == s % 2))

    def help_arrive(s):
        for h in range(2):
            ref = help_tab.at[s, pl.ds(h * half, half)]
            arrive(ref, hsend.at[s, h, 1], hrecv.at[s, h], helper & (core == s % 2))
            send(ref, ref, hsend.at[s, h, 1], hrecv.at[s, h], partner, helper & (core == s % 2))

    def help_finish(s):
        for h in range(2):
            ref = help_tab.at[s, pl.ds(h * half, half)]
            arrive(ref, hsend.at[s, h, 1], hrecv.at[s, h], helper & (core != s % 2))

    def shared_part(i):
        return shared.at[pl.ds(i * tall, tall)]

    def widen(source, target):
        for s in range(spread):
            @pl.loop(0, tables)
            def _(index):
                signs = source[s, index, :size, :].astype(jnp.bfloat16)
                target[s * tables + index] = jnp.concatenate([signs, signs], axis=1)

    for s in range(spread):
        for q in range(PIECES):
            table_stage(s, q, True)
    for j in range(PARTS_A):
        alpha_send(j, 0)
        ref = colbuf[j].at[pl.ds(r * blocks, blocks)]
        send(ref, ref, asend.at[j, chips], arecv.at[j, chips], partner)
        if j == 0:
            for i in range(PARTS_B):
                beta_send(i, 0, 0)
            for q in range(PIECES):
                for s in range(spread):
                    table_stage(s, q, False)

    out[...] = jnp.zeros_like(out)

    @pl.loop(0, tables)
    def _(index):
        signs = own_tab[index, :size, :].astype(jnp.bfloat16)
        alpha_signs[index] = jnp.concatenate([signs, signs], axis=1)

    def alpha_compute(j):
        @pl.loop(0, blocks)
        def _(block):
            total = jnp.zeros((size, wide), jnp.float32)
            for l in range(link_max):
                source = links[r * blocks + block, l]
                high, low = split(colbuf[j][source])
                index = block * link_max + l
                term = jnp.dot(alpha_signs[index], jnp.concatenate([high, low], axis=0),
                               preferred_element_type=jnp.float32)
                scale = own_tab[index, pl.ds(size, 1), :]
                scale = jnp.concatenate([scale] * (wide // size), axis=1)
                total = total + term * scale
            where = (pl.ds(pl.multiple_of(block * size, size), size), pl.ds(j * wide, wide))
            out[where] = out[where] + total

    def beta_compute(i, owner, tabs, signs, target, add):
        @pl.loop(0, blocks_b)
        def _(block):
            total = jnp.zeros((tall, size), jnp.float32)
            for l in range(link_max):
                source = links[owner * blocks_b + block, l]
                high, low = split(rowbuf[i][source])
                index = block * link_max + l
                term = lax.dot_general(
                    jnp.concatenate([high, low], axis=1), signs[index],
                    (((1,), (1,)), ((), ())), preferred_element_type=jnp.float32)
                scale = tabs[block // blocks, lax.rem(index, tables), pl.ds(size, 1), :]
                total = total + term * scale
            where = (pl.ds(i * tall, tall), pl.ds(pl.multiple_of(block * size, size), size))
            if add:
                total = target[where] + total
            target[where] = total

    for s in range(spread):
        table_finish(s)
    if helped:
        for s in range(spread):
            help_send(s)
    for i in range(PARTS_B):
        beta_send(i, 0, 1)
    widen(beta_tab, beta_signs)

    for t in range(cols - 1):
        for i in range(PARTS_B):
            beta_arrive(i, t, 0)
            if t < cols - 2:
                beta_send(i, t + 1, 0)
        if t < reach - 1:
            for j in range(PARTS_A):
                alpha_arrive(j, t)
                alpha_send(j, t + 1)
    for t in range(cols - 1, reach - 1):
        for j in range(PARTS_A):
            alpha_arrive(j, t)
            alpha_send(j, t + 1)

    def own_helped(add):
        for i in range(helped):
            @pl.when(inner)
            def _():
                beta_compute(i, c, beta_tab, beta_signs, out, add)

    own_helped(True)
    if helped:
        for s in range(spread):
            help_arrive(s)
        for s in range(spread):
            help_finish(s)

        @pl.when(helper)
        def _():
            widen(help_tab, help_signs)

        for i in range(helped):
            @pl.when(helper)
            def _():
                beta_compute(i, aided, help_tab, help_signs, shared, False)

            send(shared_part(i), shared_part(i), rsend.at[i], rrecv.at[i], (r, aided), helper)

    for j in range(PARTS_A):
        alpha_arrive(j, reach - 1)
        alpha_partner(j)
        if j % 2 == 0:
            i = helped + j // 2
            if i < PARTS_B:
                beta_arrive(i, 0, 1)
                beta_send(i, 1, 1)
        alpha_compute(j)
    for i in range(helped + (PARTS_A + 1) // 2, PARTS_B):
        beta_arrive(i, 0, 1)
        beta_send(i, 1, 1)
    for i in range(helped):
        arrive(shared_part(i), rsend.at[i], rrecv.at[i], at_end)

        @pl.when(at_end)
        def _():
            rows_here = pl.ds(i * tall, tall)
            out[rows_here, :] = out[rows_here, :] + shared[rows_here, :]

    for i in range(helped, PARTS_B):
        for t in range(1, cols - 2):
            beta_arrive(i, t, 1)
            beta_send(i, t + 1, 1)
        beta_arrive(i, cols - 2, 1)
        beta_compute(i, c, beta_tab, beta_signs, out, True)

    for cond, copy in pending:
        if cond is None:
            copy.wait_send()
        else:
            pl.when(cond)(copy.wait_send)


def local(vector, one_electron, links, counts, pairs, signs, rows, cols):
    blocks, link_max = pairs.shape
    size = signs.shape[2]
    high, width = vector.shape
    spread = rows // cols
    tables = blocks * link_max
    used = lax.dynamic_slice_in_dim(counts, lax.axis_index("row") * blocks, blocks)
    coef = pair_values(pairs, used, one_electron).reshape(tables, 1, 1)
    tab = jnp.concatenate(
        [signs.reshape(tables, size, size).astype(jnp.float32),
         jnp.broadcast_to(coef, (tables, PAD, size))], axis=1)
    chips = rows // 2
    scratch = [pltpu.VMEM((rows * blocks, size, width // PARTS_A), jnp.float32)] * PARTS_A
    scratch += [pltpu.VMEM((cols * blocks * spread, high // PARTS_B, size), jnp.float32)] * PARTS_B
    scratch += [
        pltpu.VMEM((tables, size + PAD, size), jnp.float32),
        pltpu.VMEM((spread, tables, size + PAD, size), jnp.float32),
        pltpu.VMEM((spread, tables, size + PAD, size), jnp.float32),
        pltpu.VMEM((tables, size, 2 * size), jnp.bfloat16),
        pltpu.VMEM((spread * tables, size, 2 * size), jnp.bfloat16),
        pltpu.VMEM((spread * tables, size, 2 * size), jnp.bfloat16),
        pltpu.VMEM((high // 2, width), jnp.float32),
        pltpu.SemaphoreType.DMA((PARTS_A, 2 * chips + 1)),
        pltpu.SemaphoreType.DMA((PARTS_A, 2 * chips + 1)),
        pltpu.SemaphoreType.DMA((PARTS_B, 4 * cols - 4)),
        pltpu.SemaphoreType.DMA((PARTS_B, 4 * cols - 4)),
        pltpu.SemaphoreType.DMA((spread, 2, PIECES, 4)),
        pltpu.SemaphoreType.DMA((spread, 2, PIECES)),
        pltpu.SemaphoreType.DMA((spread, 2, 2)),
        pltpu.SemaphoreType.DMA((spread, 2)),
        pltpu.SemaphoreType.DMA((PARTS_B,)),
        pltpu.SemaphoreType.DMA((PARTS_B,)),
        pltpu.SemaphoreType.DMA((PARTS_A * blocks + PARTS_B * blocks * spread + 1,)),
    ]
    return pl.pallas_call(
        functools.partial(kernel, rows, cols, blocks, link_max),
        out_shape=jax.ShapeDtypeStruct(vector.shape, jnp.float32),
        in_specs=[
            pl.BlockSpec(memory_space=pltpu.SMEM),
            pl.BlockSpec(memory_space=pl.ANY),
            pl.BlockSpec(memory_space=pl.ANY),
        ],
        out_specs=pl.BlockSpec(memory_space=pltpu.VMEM),
        scratch_shapes=scratch,
        compiler_params=pltpu.CompilerParams(
            collective_id=0, has_side_effects=True, vmem_limit_bytes=60 << 20),
    )(links, vector, tab)


def solution(mesh):
    in_specs = (P("row", "col"), P(), P(), P(), P("row", None), P("row", None, None, None))
    out_specs = P("row", "col")
    body = functools.partial(local, rows=mesh.shape["row"], cols=mesh.shape["col"])
    return jax.shard_map(body, mesh=mesh, in_specs=in_specs, out_specs=out_specs, check_vma=False)
```

```python
import functools

import jax
import jax.numpy as jnp
from jax import lax
from jax.experimental import pallas as pl
from jax.experimental.pallas import tpu as pltpu
from jax.sharding import PartitionSpec as P

MESH = pl.DeviceIdType.MESH
PARTS_A = 4
PARTS_B = 4
PAD = 8
PIECES = 4


def pair_values(pair_ids, used, integrals):
    flat_table = integrals.reshape(-1)
    onehot = pair_ids[:, :, None] == jnp.arange(flat_table.shape[0], dtype=jnp.int32)[None, None, :]
    values = jnp.sum(jnp.where(onehot, flat_table[None, None, :], 0.0), axis=2)
    in_use = jnp.arange(pair_ids.shape[1], dtype=jnp.int32)[None, :] < used[:, None]
    return jnp.where(in_use, values, 0.0)


def split(value):
    high = value.astype(jnp.bfloat16)
    low = (value - high.astype(jnp.float32)).astype(jnp.bfloat16)
    return high, low


def kernel(rows, cols, blocks, link_max, links, v, tab, out, *scratch):
    scratch = list(scratch)
    colbuf = [scratch.pop(0) for _ in range(PARTS_A)]
    rowbuf = [scratch.pop(0) for _ in range(PARTS_B)]
    own_tab, beta_tab, help_tab, alpha_signs, beta_signs, help_signs, shared = scratch[:7]
    asend, arecv, bsend, brecv, tsend, trecv, hsend, hrecv, rsend, rrecv, lsem = scratch[7:]

    size = own_tab.shape[2]
    width = out.shape[1]
    wide = width // PARTS_A
    tall = out.shape[0] // PARTS_B
    spread = rows // cols
    blocks_b = blocks * spread
    tables = blocks * link_max
    chips = rows // 2
    reach = chips // 2
    across = chips // 2
    helped = PARTS_B // 2 if cols >= 4 else 0

    r = lax.axis_index("row")
    c = lax.axis_index("col")
    core = lax.rem(r, 2)
    chip = r // 2
    other = r + 1 - 2 * core
    place = jnp.where(chip < across, chip, chips - 1 - (chip - across))

    def chip_at(position):
        position = lax.rem(position + 2 * chips, chips)
        return jnp.where(position < across, position, across + (chips - 1 - position))

    def row_at(position, k):
        return 2 * chip_at(position) + k

    right = (row_at(place + 1, core), c)
    left = (row_at(place - 1, core), c)
    partner = (other, c)
    up = (r, jnp.minimum(c + 1, cols - 1))
    down = (r, jnp.maximum(c - 1, 0))
    has_up = c < cols - 1
    has_down = c > 0
    at_end = (c == 0) | (c == cols - 1)
    inner = jnp.logical_not(at_end)
    helper = (c == 1) | (c == cols - 2)
    aided = jnp.where(c == 1, 0, cols - 1)
    inward = jnp.where(c == 0, 1, cols - 2)

    barrier = pltpu.get_barrier_semaphore()
    for device in (right, left, partner):
        pl.semaphore_signal(barrier, inc=1, device_id=device, device_id_type=MESH)

    @pl.when(has_up)
    def _():
        pl.semaphore_signal(barrier, inc=1, device_id=up, device_id_type=MESH)

    @pl.when(has_down)
    def _():
        pl.semaphore_signal(barrier, inc=1, device_id=down, device_id_type=MESH)

    loads = []
    for j in range(PARTS_A):
        for i in range(blocks):
            loads.append(pltpu.make_async_copy(
                v.at[pl.ds(i * size, size), pl.ds(j * wide, wide)],
                colbuf[j].at[r * blocks + i], lsem.at[len(loads)]))
    for i in range(PARTS_B):
        for k in range(blocks_b):
            loads.append(pltpu.make_async_copy(
                v.at[pl.ds(i * tall, tall), pl.ds(k * size, size)],
                rowbuf[i].at[c * blocks_b + k], lsem.at[len(loads)]))
    loads.append(pltpu.make_async_copy(tab, own_tab, lsem.at[len(loads)]))
    for load in loads:
        load.start()
    for load in loads:
        load.wait()

    pl.semaphore_wait(barrier, 3 + has_up.astype(jnp.int32) + has_down.astype(jnp.int32))

    pending = []

    def send(src, dst, ssem, rsem, device, cond=None):
        copy = pltpu.make_async_remote_copy(
            src_ref=src, dst_ref=dst, send_sem=ssem, recv_sem=rsem,
            device_id=device, device_id_type=MESH)
        pending.append((cond, copy))
        if cond is None:
            copy.start()
        else:
            pl.when(cond)(copy.start)

    def arrive(ref, ssem, rsem, cond=None):
        copy = pltpu.make_async_remote_copy(
            src_ref=ref, dst_ref=ref, send_sem=ssem, recv_sem=rsem,
            device_id=partner, device_id_type=MESH)
        if cond is None:
            copy.wait_recv()
        else:
            pl.when(cond)(copy.wait_recv)

    def alpha_part(j, position, k, t, leftward):
        start = row_at(position, k) * blocks
        count = blocks
        if t == reach - 1:
            count = blocks // 2
            if leftward:
                start = start + count
        return colbuf[j].at[pl.ds(start, count)]

    def alpha_send(j, t):
        ref = alpha_part(j, place - t, core, t, False)
        send(ref, ref, asend.at[j, t], arecv.at[j, t], right)
        ref = alpha_part(j, place + t, core, t, True)
        send(ref, ref, asend.at[j, reach + t], arecv.at[j, reach + t], left)

    def alpha_arrive(j, t):
        m = chips + 1 + t
        ref = alpha_part(j, place - 1 - t, core, t, False)
        arrive(ref, asend.at[j, t], arecv.at[j, t])
        send(ref, ref, asend.at[j, m], arecv.at[j, m], partner)
        m = m + reach
        ref = alpha_part(j, place + 1 + t, core, t, True)
        arrive(ref, asend.at[j, reach + t], arecv.at[j, reach + t])
        send(ref, ref, asend.at[j, m], arecv.at[j, m], partner)

    def alpha_partner(j):
        m = chips
        ref = colbuf[j].at[pl.ds(other * blocks, blocks)]
        arrive(ref, asend.at[j, m], arecv.at[j, m])
        for t in range(reach):
            m = chips + 1 + t
            arrive(alpha_part(j, place - 1 - t, 1 - core, t, False), asend.at[j, m], arecv.at[j, m])
            m = m + reach
            arrive(alpha_part(j, place + 1 + t, 1 - core, t, True), asend.at[j, m], arecv.at[j, m])

    def beta_part(i, tile):
        return rowbuf[i].at[pl.ds(jnp.clip(tile, 0, cols - 1) * blocks_b, blocks_b)]

    def in_turn(i, tile, late):
        if i < helped or helped == 0:
            return jnp.bool_(not late) & (tile >= 0) & (tile < cols)
        from_end = (tile == 0) | (tile == cols - 1)
        return from_end if late else (tile > 0) & (tile < cols - 1)

    def beta_send(i, t, late):
        if late and (i < helped or helped == 0):
            return
        above = has_up & in_turn(i, c - t, late)
        below = has_down & in_turn(i, c + t, late)
        if i < helped:
            above = above & (c + 1 < cols - 1)
            below = below & (c - 1 > 0)
        ref = beta_part(i, c - t)
        m = 2 * late * (cols - 1) + t
        send(ref, ref, bsend.at[i, m], brecv.at[i, m], up, above)
        ref = beta_part(i, c + t)
        m = m + cols - 1
        send(ref, ref, bsend.at[i, m], brecv.at[i, m], down, below)

    def beta_arrive(i, t, late):
        if late and (i < helped or helped == 0):
            return
        above = in_turn(i, c - 1 - t, late)
        below = in_turn(i, c + 1 + t, late)
        if i < helped:
            above = above & inner
            below = below & inner
        m = 2 * late * (cols - 1) + t
        arrive(beta_part(i, c - 1 - t), bsend.at[i, m], brecv.at[i, m], above)
        m = m + cols - 1
        arrive(beta_part(i, c + 1 + t), bsend.at[i, m], brecv.at[i, m], below)

    def table_places(s):
        source = c * spread + s
        source_chip = source // 2
        source_place = jnp.where(
            source_chip < across, source_chip, chips - 1 - (source_chip - across))
        distance = lax.rem(place - source_place + chips, chips)
        return lax.rem(source, 2), distance

    piece = tables // (2 * PIECES)

    def table_stage(s, q, d):
        source_core, distance = table_places(s)
        for h in range(2):
            hops = distance if h == 0 else lax.rem(chips - distance, chips)
            here = (core == source_core) & (hops == d)
            part = pl.ds((h * PIECES + q) * piece, piece)
            ref = beta_tab.at[s, part]
            src = ref if d else own_tab.at[part]
            if d:
                arrive(ref, tsend.at[s, h, q, 0], trecv.at[s, h, q], here)
            if d + 1 < chips:
                send(src, ref, tsend.at[s, h, q, 0], trecv.at[s, h, q],
                     right if h == 0 else left, here)
            send(src, ref, tsend.at[s, h, q, 1], trecv.at[s, h, q], partner, here)

    def table_finish(s):
        source_core, distance = table_places(s)
        mine = core == source_core
        for q in range(PIECES):
            for h in range(2):
                ref = beta_tab.at[s, pl.ds((h * PIECES + q) * piece, piece)]
                arrive(ref, tsend.at[s, h, q, 0], trecv.at[s, h, q], jnp.logical_not(mine))

        @pl.when(mine & (distance == 0))
        def _():
            copy = pltpu.make_async_copy(own_tab, beta_tab.at[s], lsem.at[0])
            copy.start()
            copy.wait()

    half = tables // 2

    def help_send(s):
        for h in range(2):
            ref = pl.ds(h * half, half)
            send(beta_tab.at[s, ref], help_tab.at[s, ref], hsend.at[s, h, 0], hrecv.at[s, h],
                 (r, inward), at_end & (core == s % 2))

    def help_arrive(s):
        for h in range(2):
            ref = help_tab.at[s, pl.ds(h * half, half)]
            arrive(ref, hsend.at[s, h, 1], hrecv.at[s, h], helper & (core == s % 2))
            send(ref, ref, hsend.at[s, h, 1], hrecv.at[s, h], partner, helper & (core == s % 2))

    def help_finish(s):
        for h in range(2):
            ref = help_tab.at[s, pl.ds(h * half, half)]
            arrive(ref, hsend.at[s, h, 1], hrecv.at[s, h], helper & (core != s % 2))

    def shared_part(i):
        return shared.at[pl.ds(i * tall, tall)]

    def widen(source, target):
        for s in range(spread):
            @pl.loop(0, tables)
            def _(index):
                signs = source[s, index, :size, :].astype(jnp.bfloat16)
                target[s * tables + index] = jnp.concatenate([signs, signs], axis=1)

    for s in range(spread):
        for q in range(PIECES):
            table_stage(s, q, 0)
    for j in range(PARTS_A):
        alpha_send(j, 0)
        ref = colbuf[j].at[pl.ds(r * blocks, blocks)]
        send(ref, ref, asend.at[j, chips], arecv.at[j, chips], partner)
        if j == 0:
            for i in range(PARTS_B):
                beta_send(i, 0, 0)
            for wave in range(PIECES + chips - 2):
                for q in range(PIECES):
                    if 1 <= wave - q + 1 < chips:
                        for s in range(spread):
                            table_stage(s, q, wave - q + 1)

    out[...] = jnp.zeros_like(out)

    @pl.loop(0, tables)
    def _(index):
        signs = own_tab[index, :size, :].astype(jnp.bfloat16)
        alpha_signs[index] = jnp.concatenate([signs, signs], axis=1)

    def alpha_compute(j):
        @pl.loop(0, blocks)
        def _(block):
            total = jnp.zeros((size, wide), jnp.float32)
            for l in range(link_max):
                source = links[r * blocks + block, l]
                high, low = split(colbuf[j][source])
                index = block * link_max + l
                term = jnp.dot(alpha_signs[index], jnp.concatenate([high, low], axis=0),
                               preferred_element_type=jnp.float32)
                scale = own_tab[index, pl.ds(size, 1), :]
                scale = jnp.concatenate([scale] * (wide // size), axis=1)
                total = total + term * scale
            where = (pl.ds(pl.multiple_of(block * size, size), size), pl.ds(j * wide, wide))
            out[where] = out[where] + total

    def beta_compute(i, owner, tabs, signs, target, add):
        @pl.loop(0, blocks_b)
        def _(block):
            total = jnp.zeros((tall, size), jnp.float32)
            for l in range(link_max):
                source = links[owner * blocks_b + block, l]
                high, low = split(rowbuf[i][source])
                index = block * link_max + l
                term = lax.dot_general(
                    jnp.concatenate([high, low], axis=1), signs[index],
                    (((1,), (1,)), ((), ())), preferred_element_type=jnp.float32)
                scale = tabs[block // blocks, lax.rem(index, tables), pl.ds(size, 1), :]
                total = total + term * scale
            where = (pl.ds(i * tall, tall), pl.ds(pl.multiple_of(block * size, size), size))
            if add:
                total = target[where] + total
            target[where] = total

    for s in range(spread):
        table_finish(s)
    if helped:
        for s in range(spread):
            help_send(s)
    for i in range(PARTS_B):
        beta_send(i, 0, 1)
    widen(beta_tab, beta_signs)

    for t in range(cols - 1):
        for i in range(PARTS_B):
            beta_arrive(i, t, 0)
            if t < cols - 2:
                beta_send(i, t + 1, 0)
        if t < reach - 1:
            for j in range(PARTS_A):
                alpha_arrive(j, t)
                alpha_send(j, t + 1)
    for t in range(cols - 1, reach - 1):
        for j in range(PARTS_A):
            alpha_arrive(j, t)
            alpha_send(j, t + 1)

    def own_helped(add):
        for i in range(helped):
            @pl.when(inner)
            def _():
                beta_compute(i, c, beta_tab, beta_signs, out, add)

    own_helped(True)
    if helped:
        for s in range(spread):
            help_arrive(s)
        for s in range(spread):
            help_finish(s)

        @pl.when(helper)
        def _():
            widen(help_tab, help_signs)

        for i in range(helped):
            @pl.when(helper)
            def _():
                beta_compute(i, aided, help_tab, help_signs, shared, False)

            send(shared_part(i), shared_part(i), rsend.at[i], rrecv.at[i], (r, aided), helper)

    for j in range(PARTS_A):
        alpha_arrive(j, reach - 1)
        alpha_partner(j)
        if j % 2 == 0:
            i = helped + j // 2
            if i < PARTS_B:
                beta_arrive(i, 0, 1)
                beta_send(i, 1, 1)
        alpha_compute(j)
    for i in range(helped + (PARTS_A + 1) // 2, PARTS_B):
        beta_arrive(i, 0, 1)
        beta_send(i, 1, 1)
    for i in range(helped):
        arrive(shared_part(i), rsend.at[i], rrecv.at[i], at_end)

        @pl.when(at_end)
        def _():
            rows_here = pl.ds(i * tall, tall)
            out[rows_here, :] = out[rows_here, :] + shared[rows_here, :]

    for i in range(helped, PARTS_B):
        for t in range(1, cols - 2):
            beta_arrive(i, t, 1)
            beta_send(i, t + 1, 1)
        beta_arrive(i, cols - 2, 1)
        beta_compute(i, c, beta_tab, beta_signs, out, True)

    for cond, copy in pending:
        if cond is None:
            copy.wait_send()
        else:
            pl.when(cond)(copy.wait_send)


def local(vector, one_electron, links, counts, pairs, signs, rows, cols):
    blocks, link_max = pairs.shape
    size = signs.shape[2]
    high, width = vector.shape
    spread = rows // cols
    tables = blocks * link_max
    used = lax.dynamic_slice_in_dim(counts, lax.axis_index("row") * blocks, blocks)
    coef = pair_values(pairs, used, one_electron).reshape(tables, 1, 1)
    tab = jnp.concatenate(
        [signs.reshape(tables, size, size).astype(jnp.float32),
         jnp.broadcast_to(coef, (tables, PAD, size))], axis=1)
    chips = rows // 2
    scratch = [pltpu.VMEM((rows * blocks, size, width // PARTS_A), jnp.float32)] * PARTS_A
    scratch += [pltpu.VMEM((cols * blocks * spread, high // PARTS_B, size), jnp.float32)] * PARTS_B
    scratch += [
        pltpu.VMEM((tables, size + PAD, size), jnp.float32),
        pltpu.VMEM((spread, tables, size + PAD, size), jnp.float32),
        pltpu.VMEM((spread, tables, size + PAD, size), jnp.float32),
        pltpu.VMEM((tables, size, 2 * size), jnp.bfloat16),
        pltpu.VMEM((spread * tables, size, 2 * size), jnp.bfloat16),
        pltpu.VMEM((spread * tables, size, 2 * size), jnp.bfloat16),
        pltpu.VMEM((high // 2, width), jnp.float32),
        pltpu.SemaphoreType.DMA((PARTS_A, 2 * chips + 1)),
        pltpu.SemaphoreType.DMA((PARTS_A, 2 * chips + 1)),
        pltpu.SemaphoreType.DMA((PARTS_B, 4 * cols - 4)),
        pltpu.SemaphoreType.DMA((PARTS_B, 4 * cols - 4)),
        pltpu.SemaphoreType.DMA((spread, 2, PIECES, 2)),
        pltpu.SemaphoreType.DMA((spread, 2, PIECES)),
        pltpu.SemaphoreType.DMA((spread, 2, 2)),
        pltpu.SemaphoreType.DMA((spread, 2)),
        pltpu.SemaphoreType.DMA((PARTS_B,)),
        pltpu.SemaphoreType.DMA((PARTS_B,)),
        pltpu.SemaphoreType.DMA((PARTS_A * blocks + PARTS_B * blocks * spread + 1,)),
    ]
    return pl.pallas_call(
        functools.partial(kernel, rows, cols, blocks, link_max),
        out_shape=jax.ShapeDtypeStruct(vector.shape, jnp.float32),
        in_specs=[
            pl.BlockSpec(memory_space=pltpu.SMEM),
            pl.BlockSpec(memory_space=pl.ANY),
            pl.BlockSpec(memory_space=pl.ANY),
        ],
        out_specs=pl.BlockSpec(memory_space=pltpu.VMEM),
        scratch_shapes=scratch,
        compiler_params=pltpu.CompilerParams(
            collective_id=0, has_side_effects=True, vmem_limit_bytes=60 << 20),
    )(links, vector, tab)


def solution(mesh):
    in_specs = (P("row", "col"), P(), P(), P(), P("row", None), P("row", None, None, None))
    out_specs = P("row", "col")
    body = functools.partial(local, rows=mesh.shape["row"], cols=mesh.shape["col"])
    return jax.shard_map(body, mesh=mesh, in_specs=in_specs, out_specs=out_specs, check_vma=False)
```

```python
import functools

import jax
import jax.numpy as jnp
from jax import lax
from jax.experimental import pallas as pl
from jax.experimental.pallas import tpu as pltpu
from jax.sharding import PartitionSpec as P

MESH = pl.DeviceIdType.MESH
PARTS_A = 4
PARTS_B = 4
PAD = 8
PIECES = 4


def pair_values(pair_ids, used, integrals):
    flat_table = integrals.reshape(-1)
    onehot = pair_ids[:, :, None] == jnp.arange(flat_table.shape[0], dtype=jnp.int32)[None, None, :]
    values = jnp.sum(jnp.where(onehot, flat_table[None, None, :], 0.0), axis=2)
    in_use = jnp.arange(pair_ids.shape[1], dtype=jnp.int32)[None, :] < used[:, None]
    return jnp.where(in_use, values, 0.0)


def split(value):
    high = value.astype(jnp.bfloat16)
    low = (value - high.astype(jnp.float32)).astype(jnp.bfloat16)
    return high, low


def kernel(rows, cols, blocks, link_max, links, v, tab, out, *scratch):
    scratch = list(scratch)
    colbuf = [scratch.pop(0) for _ in range(PARTS_A)]
    rowbuf = [scratch.pop(0) for _ in range(PARTS_B)]
    own_tab, beta_tab, help_tab, alpha_signs, beta_signs, help_signs, shared = scratch[:7]
    asend, arecv, bsend, brecv, tsend, trecv, hsend, hrecv, rsend, rrecv, lsem = scratch[7:]

    size = own_tab.shape[2]
    width = out.shape[1]
    wide = width // PARTS_A
    tall = out.shape[0] // PARTS_B
    spread = rows // cols
    blocks_b = blocks * spread
    tables = blocks * link_max
    chips = rows // 2
    reach = chips // 2
    across = chips // 2
    helped = PARTS_B // 2 if cols >= 4 else 0

    r = lax.axis_index("row")
    c = lax.axis_index("col")
    core = lax.rem(r, 2)
    chip = r // 2
    other = r + 1 - 2 * core
    place = jnp.where(chip < across, chip, chips - 1 - (chip - across))

    def chip_at(position):
        position = lax.rem(position + 2 * chips, chips)
        return jnp.where(position < across, position, across + (chips - 1 - position))

    def row_at(position, k):
        return 2 * chip_at(position) + k

    right = (row_at(place + 1, core), c)
    left = (row_at(place - 1, core), c)
    partner = (other, c)
    up = (r, jnp.minimum(c + 1, cols - 1))
    down = (r, jnp.maximum(c - 1, 0))
    has_up = c < cols - 1
    has_down = c > 0
    at_end = (c == 0) | (c == cols - 1)
    inner = jnp.logical_not(at_end)
    helper = (c == 1) | (c == cols - 2)
    aided = jnp.where(c == 1, 0, cols - 1)
    inward = jnp.where(c == 0, 1, cols - 2)

    barrier = pltpu.get_barrier_semaphore()
    for device in (right, left, partner):
        pl.semaphore_signal(barrier, inc=1, device_id=device, device_id_type=MESH)

    @pl.when(has_up)
    def _():
        pl.semaphore_signal(barrier, inc=1, device_id=up, device_id_type=MESH)

    @pl.when(has_down)
    def _():
        pl.semaphore_signal(barrier, inc=1, device_id=down, device_id_type=MESH)

    loads = []
    for j in range(PARTS_A):
        for i in range(blocks):
            loads.append(pltpu.make_async_copy(
                v.at[pl.ds(i * size, size), pl.ds(j * wide, wide)],
                colbuf[j].at[r * blocks + i], lsem.at[len(loads)]))
    for i in range(PARTS_B):
        for k in range(blocks_b):
            loads.append(pltpu.make_async_copy(
                v.at[pl.ds(i * tall, tall), pl.ds(k * size, size)],
                rowbuf[i].at[c * blocks_b + k], lsem.at[len(loads)]))
    loads.append(pltpu.make_async_copy(tab, own_tab, lsem.at[len(loads)]))
    for load in loads:
        load.start()
    for load in loads:
        load.wait()

    pl.semaphore_wait(barrier, 3 + has_up.astype(jnp.int32) + has_down.astype(jnp.int32))

    pending = []

    def send(src, dst, ssem, rsem, device, cond=None):
        copy = pltpu.make_async_remote_copy(
            src_ref=src, dst_ref=dst, send_sem=ssem, recv_sem=rsem,
            device_id=device, device_id_type=MESH)
        pending.append((cond, copy))
        if cond is None:
            copy.start()
        else:
            pl.when(cond)(copy.start)

    def arrive(ref, ssem, rsem, cond=None):
        copy = pltpu.make_async_remote_copy(
            src_ref=ref, dst_ref=ref, send_sem=ssem, recv_sem=rsem,
            device_id=partner, device_id_type=MESH)
        if cond is None:
            copy.wait_recv()
        else:
            pl.when(cond)(copy.wait_recv)

    def alpha_part(j, position, k, t, leftward):
        start = row_at(position, k) * blocks
        count = blocks
        if t == reach - 1:
            count = blocks // 2
            if leftward:
                start = start + count
        return colbuf[j].at[pl.ds(start, count)]

    def alpha_send(j, t):
        ref = alpha_part(j, place - t, core, t, False)
        send(ref, ref, asend.at[j, t], arecv.at[j, t], right)
        ref = alpha_part(j, place + t, core, t, True)
        send(ref, ref, asend.at[j, reach + t], arecv.at[j, reach + t], left)

    def alpha_arrive(j, t):
        m = chips + 1 + t
        ref = alpha_part(j, place - 1 - t, core, t, False)
        arrive(ref, asend.at[j, t], arecv.at[j, t])
        send(ref, ref, asend.at[j, m], arecv.at[j, m], partner)
        m = m + reach
        ref = alpha_part(j, place + 1 + t, core, t, True)
        arrive(ref, asend.at[j, reach + t], arecv.at[j, reach + t])
        send(ref, ref, asend.at[j, m], arecv.at[j, m], partner)

    def alpha_partner(j):
        m = chips
        ref = colbuf[j].at[pl.ds(other * blocks, blocks)]
        arrive(ref, asend.at[j, m], arecv.at[j, m])
        for t in range(reach):
            m = chips + 1 + t
            arrive(alpha_part(j, place - 1 - t, 1 - core, t, False), asend.at[j, m], arecv.at[j, m])
            m = m + reach
            arrive(alpha_part(j, place + 1 + t, 1 - core, t, True), asend.at[j, m], arecv.at[j, m])

    def beta_part(i, tile):
        return rowbuf[i].at[pl.ds(jnp.clip(tile, 0, cols - 1) * blocks_b, blocks_b)]

    def in_turn(i, tile, late):
        if i < helped or helped == 0:
            return jnp.bool_(not late) & (tile >= 0) & (tile < cols)
        from_end = (tile == 0) | (tile == cols - 1)
        return from_end if late else (tile > 0) & (tile < cols - 1)

    def beta_send(i, t, late):
        if late and (i < helped or helped == 0):
            return
        above = has_up & in_turn(i, c - t, late)
        below = has_down & in_turn(i, c + t, late)
        if i < helped:
            above = above & (c + 1 < cols - 1)
            below = below & (c - 1 > 0)
        ref = beta_part(i, c - t)
        m = 2 * late * (cols - 1) + t
        send(ref, ref, bsend.at[i, m], brecv.at[i, m], up, above)
        ref = beta_part(i, c + t)
        m = m + cols - 1
        send(ref, ref, bsend.at[i, m], brecv.at[i, m], down, below)

    def beta_arrive(i, t, late):
        if late and (i < helped or helped == 0):
            return
        above = in_turn(i, c - 1 - t, late)
        below = in_turn(i, c + 1 + t, late)
        if i < helped:
            above = above & inner
            below = below & inner
        m = 2 * late * (cols - 1) + t
        arrive(beta_part(i, c - 1 - t), bsend.at[i, m], brecv.at[i, m], above)
        m = m + cols - 1
        arrive(beta_part(i, c + 1 + t), bsend.at[i, m], brecv.at[i, m], below)

    def table_places(s):
        source = c * spread + s
        source_chip = source // 2
        source_place = jnp.where(
            source_chip < across, source_chip, chips - 1 - (source_chip - across))
        distance = lax.rem(place - source_place + chips, chips)
        return lax.rem(source, 2), distance

    piece = tables // (2 * PIECES)

    def table_stage(s, q, d):
        source_core, distance = table_places(s)
        for h in range(2):
            hops = distance if h == 0 else lax.rem(chips - distance, chips)
            here = (core == source_core) & (hops == d)
            part = pl.ds((h * PIECES + q) * piece, piece)
            ref = beta_tab.at[s, part]
            src = ref if d else own_tab.at[part]
            if d:
                arrive(ref, tsend.at[s, h, q, 0], trecv.at[s, h, q], here)
            if d + 1 < chips:
                send(src, ref, tsend.at[s, h, q, 0], trecv.at[s, h, q],
                     right if h == 0 else left, here)
            send(src, ref, tsend.at[s, h, q, 1], trecv.at[s, h, q], partner, here)

    def table_finish(s):
        source_core, distance = table_places(s)
        mine = core == source_core
        for q in range(PIECES):
            for h in range(2):
                ref = beta_tab.at[s, pl.ds((h * PIECES + q) * piece, piece)]
                arrive(ref, tsend.at[s, h, q, 0], trecv.at[s, h, q], jnp.logical_not(mine))

        @pl.when(mine & (distance == 0))
        def _():
            copy = pltpu.make_async_copy(own_tab, beta_tab.at[s], lsem.at[0])
            copy.start()
            copy.wait()

    half = tables // 2

    def help_send(s):
        for h in range(2):
            ref = pl.ds(h * half, half)
            send(beta_tab.at[s, ref], help_tab.at[s, ref], hsend.at[s, h, 0], hrecv.at[s, h],
                 (r, inward), at_end & (core == s % 2))

    def help_arrive(s):
        for h in range(2):
            ref = help_tab.at[s, pl.ds(h * half, half)]
            arrive(ref, hsend.at[s, h, 1], hrecv.at[s, h], helper & (core == s % 2))
            send(ref, ref, hsend.at[s, h, 1], hrecv.at[s, h], partner, helper & (core == s % 2))

    def help_finish(s):
        for h in range(2):
            ref = help_tab.at[s, pl.ds(h * half, half)]
            arrive(ref, hsend.at[s, h, 1], hrecv.at[s, h], helper & (core != s % 2))

    def shared_part(i):
        return shared.at[pl.ds(i * tall, tall)]

    def widen(source, target):
        for s in range(spread):
            @pl.loop(0, tables)
            def _(index):
                signs = source[s, index, :size, :].astype(jnp.bfloat16)
                target[s * tables + index] = jnp.concatenate([signs, signs], axis=1)

    for s in range(spread):
        for q in range(PIECES):
            table_stage(s, q, 0)
    for j in range(PARTS_A):
        alpha_send(j, 0)
        ref = colbuf[j].at[pl.ds(r * blocks, blocks)]
        send(ref, ref, asend.at[j, chips], arecv.at[j, chips], partner)
        if j == 0:
            for i in range(PARTS_B):
                beta_send(i, 0, 0)
                beta_send(i, 0, 1)
            for wave in range(PIECES + chips - 2):
                for q in range(PIECES):
                    if 1 <= wave - q + 1 < chips:
                        for s in range(spread):
                            table_stage(s, q, wave - q + 1)

    out[...] = jnp.zeros_like(out)

    @pl.loop(0, tables)
    def _(index):
        signs = own_tab[index, :size, :].astype(jnp.bfloat16)
        alpha_signs[index] = jnp.concatenate([signs, signs], axis=1)

    def alpha_compute(j):
        @pl.loop(0, blocks)
        def _(block):
            total = jnp.zeros((size, wide), jnp.float32)
            for l in range(link_max):
                source = links[r * blocks + block, l]
                high, low = split(colbuf[j][source])
                index = block * link_max + l
                term = jnp.dot(alpha_signs[index], jnp.concatenate([high, low], axis=0),
                               preferred_element_type=jnp.float32)
                scale = own_tab[index, pl.ds(size, 1), :]
                scale = jnp.concatenate([scale] * (wide // size), axis=1)
                total = total + term * scale
            where = (pl.ds(pl.multiple_of(block * size, size), size), pl.ds(j * wide, wide))
            out[where] = out[where] + total

    def beta_compute(i, owner, tabs, signs, target, add):
        @pl.loop(0, blocks_b)
        def _(block):
            total = jnp.zeros((tall, size), jnp.float32)
            for l in range(link_max):
                source = links[owner * blocks_b + block, l]
                high, low = split(rowbuf[i][source])
                index = block * link_max + l
                term = lax.dot_general(
                    jnp.concatenate([high, low], axis=1), signs[index],
                    (((1,), (1,)), ((), ())), preferred_element_type=jnp.float32)
                scale = tabs[block // blocks, lax.rem(index, tables), pl.ds(size, 1), :]
                total = total + term * scale
            where = (pl.ds(i * tall, tall), pl.ds(pl.multiple_of(block * size, size), size))
            if add:
                total = target[where] + total
            target[where] = total

    for s in range(spread):
        table_finish(s)
    if helped:
        for s in range(spread):
            help_send(s)
    widen(beta_tab, beta_signs)

    for t in range(cols - 1):
        for i in range(PARTS_B):
            beta_arrive(i, t, 0)
            if t < cols - 2:
                beta_send(i, t + 1, 0)
        if t < reach - 1:
            for j in range(PARTS_A):
                alpha_arrive(j, t)
                alpha_send(j, t + 1)
    for t in range(cols - 1, reach - 1):
        for j in range(PARTS_A):
            alpha_arrive(j, t)
            alpha_send(j, t + 1)

    def own_helped(add):
        for i in range(helped):
            @pl.when(inner)
            def _():
                beta_compute(i, c, beta_tab, beta_signs, out, add)

    for i in range(helped, PARTS_B):
        beta_arrive(i, 0, 1)
        beta_send(i, 1, 1)
    own_helped(True)
    for t in range(1, cols - 2):
        for i in range(helped, PARTS_B):
            beta_arrive(i, t, 1)
            beta_send(i, t + 1, 1)
    if helped:
        for s in range(spread):
            help_arrive(s)
        for s in range(spread):
            help_finish(s)

        @pl.when(helper)
        def _():
            widen(help_tab, help_signs)

        for i in range(helped):
            @pl.when(helper)
            def _():
                beta_compute(i, aided, help_tab, help_signs, shared, False)

            send(shared_part(i), shared_part(i), rsend.at[i], rrecv.at[i], (r, aided), helper)

    for j in range(PARTS_A):
        alpha_arrive(j, reach - 1)
        alpha_partner(j)
        alpha_compute(j)
    for i in range(helped):
        arrive(shared_part(i), rsend.at[i], rrecv.at[i], at_end)

        @pl.when(at_end)
        def _():
            rows_here = pl.ds(i * tall, tall)
            out[rows_here, :] = out[rows_here, :] + shared[rows_here, :]

    for i in range(helped, PARTS_B):
        beta_arrive(i, cols - 2, 1)
        beta_compute(i, c, beta_tab, beta_signs, out, True)

    for cond, copy in pending:
        if cond is None:
            copy.wait_send()
        else:
            pl.when(cond)(copy.wait_send)


def local(vector, one_electron, links, counts, pairs, signs, rows, cols):
    blocks, link_max = pairs.shape
    size = signs.shape[2]
    high, width = vector.shape
    spread = rows // cols
    tables = blocks * link_max
    used = lax.dynamic_slice_in_dim(counts, lax.axis_index("row") * blocks, blocks)
    coef = pair_values(pairs, used, one_electron).reshape(tables, 1, 1)
    tab = jnp.concatenate(
        [signs.reshape(tables, size, size).astype(jnp.float32),
         jnp.broadcast_to(coef, (tables, PAD, size))], axis=1)
    chips = rows // 2
    scratch = [pltpu.VMEM((rows * blocks, size, width // PARTS_A), jnp.float32)] * PARTS_A
    scratch += [pltpu.VMEM((cols * blocks * spread, high // PARTS_B, size), jnp.float32)] * PARTS_B
    scratch += [
        pltpu.VMEM((tables, size + PAD, size), jnp.float32),
        pltpu.VMEM((spread, tables, size + PAD, size), jnp.float32),
        pltpu.VMEM((spread, tables, size + PAD, size), jnp.float32),
        pltpu.VMEM((tables, size, 2 * size), jnp.bfloat16),
        pltpu.VMEM((spread * tables, size, 2 * size), jnp.bfloat16),
        pltpu.VMEM((spread * tables, size, 2 * size), jnp.bfloat16),
        pltpu.VMEM((high // 2, width), jnp.float32),
        pltpu.SemaphoreType.DMA((PARTS_A, 2 * chips + 1)),
        pltpu.SemaphoreType.DMA((PARTS_A, 2 * chips + 1)),
        pltpu.SemaphoreType.DMA((PARTS_B, 4 * cols - 4)),
        pltpu.SemaphoreType.DMA((PARTS_B, 4 * cols - 4)),
        pltpu.SemaphoreType.DMA((spread, 2, PIECES, 2)),
        pltpu.SemaphoreType.DMA((spread, 2, PIECES)),
        pltpu.SemaphoreType.DMA((spread, 2, 2)),
        pltpu.SemaphoreType.DMA((spread, 2)),
        pltpu.SemaphoreType.DMA((PARTS_B,)),
        pltpu.SemaphoreType.DMA((PARTS_B,)),
        pltpu.SemaphoreType.DMA((PARTS_A * blocks + PARTS_B * blocks * spread + 1,)),
    ]
    return pl.pallas_call(
        functools.partial(kernel, rows, cols, blocks, link_max),
        out_shape=jax.ShapeDtypeStruct(vector.shape, jnp.float32),
        in_specs=[
            pl.BlockSpec(memory_space=pltpu.SMEM),
            pl.BlockSpec(memory_space=pl.ANY),
            pl.BlockSpec(memory_space=pl.ANY),
        ],
        out_specs=pl.BlockSpec(memory_space=pltpu.VMEM),
        scratch_shapes=scratch,
        compiler_params=pltpu.CompilerParams(
            collective_id=0, has_side_effects=True, vmem_limit_bytes=60 << 20),
    )(links, vector, tab)


def solution(mesh):
    in_specs = (P("row", "col"), P(), P(), P(), P("row", None), P("row", None, None, None))
    out_specs = P("row", "col")
    body = functools.partial(local, rows=mesh.shape["row"], cols=mesh.shape["col"])
    return jax.shard_map(body, mesh=mesh, in_specs=in_specs, out_specs=out_specs, check_vma=False)
```
